512 devices in a mesh: band: 8 (over y, core), exp: 64 (over x, z).
Axes of the slice: x: 4, y: 4, z: 16, core: 2. Of those that a mesh axis runs over, the one named last changes fastest.
Arguments:
- exposure: float32 [524288, 512], P(('band', 'exp')), parts along dimension 0, may hold values from -8 to 8, as said below
- psf_taps: bfloat16 [512, 15], P(('band', 'exp')), parts along dimension 0, may hold values from -1.5 to 1.5
- col_warp: bfloat16 [262144, 512], P(('band', 'exp')), parts along dimension 0, may hold values from -0.25 to 0.25
- row_warp: bfloat16 [262144, 1024], P(('band', 'exp')), parts along dimension 0, may hold values from -0.1875 to 0.1875
- row_patch: int32 [262144, 1], P(('band', 'exp')), parts along dimension 0, may hold values from 0 to 63; in each aligned block of 512 rows (0 to 511, 512 to 1023, ...) at most 16 rows name the same one
- row_prow: int32 [262144], P(('band', 'exp')), parts along dimension 0, may hold values from 0 to 31
- owner_map: int32 [512], P('band'), parts along dimension 0, may hold values from 0 to 63, each once
Outputs:
- coadd: float32 [16384, 512], P(('band', 'exp')), parts along dimension 0
The draws below stay inside these ranges and needn't reach their ends.
There are 8 independent parts, one for each index of `band`. The reference program is written for one: setup_inputs(seed, part) draws one part's arguments, and reference() takes and returns one part's arrays. A program takes and returns all parts, laid end to end along the dimension named above; each array names one. Nothing has to cross between parts.
Inputs may be any that keep to these rules, and one draw needn't show every extreme that they name: `row_patch`: the 512 resampled rows of one exposure piece (aligned blocks) name any one patch at most 16 times, a bound that some block reaches. `exposure`: each piece carries a background level per block of 128 columns on top of the sky noise.
All inputs are finite; a program needn't handle non-finite values.
Results may differ from the reference program's by a relative error of at most 0.0051.
Values sent between devices are 32-bit elements; how exact they have to be, the bound alone decides.
A program may use at most 64 MiB of HBM per device.

```python
import math
import jax
import jax.numpy as jnp
import numpy as np
from jax import lax

W = 512
R = 1024
STRIP = 16
TAPS = 15
PATCH_ROWS = 32
RO = 512
EXPOSURES = 64
NPATCH = 64
ROWS = 65536
OUT_ROWS = 32768
CAP = 16


def draw_exposure(key, part):
    noise_key, level_key = jax.random.split(jax.random.fold_in(key, 11))
    noise = jnp.clip(jax.random.normal(noise_key, (ROWS, W), jnp.float32), -5.0, 5.0)
    levels = jax.random.uniform(level_key, (EXPOSURES, W // 128), jnp.float32, -2.0, 2.0)
    full = jnp.repeat(jnp.repeat(levels, 128, axis=1), R, axis=0)
    return noise + full


def with_ends(values, stream_key, low, top_value):
    longest = values.shape.index(max(values.shape))
    spots = []
    for shift in (0, 1):
        where = [jax.random.randint(jax.random.fold_in(stream_key, axis), (), 0, length) for axis, length in enumerate(values.shape)]
        where[longest] = (where[longest] + shift) % values.shape[longest]
        spots.append(tuple(where))
    return values.at[spots[0]].set(low).at[spots[1]].set(top_value)


def block_levels(stream_key, dims, shards, least, high):
    def one(axis_at, blocks):
        draws = jax.random.uniform(jax.random.fold_in(jax.random.fold_in(stream_key, 6), axis_at), (blocks,), jnp.float32, least / len(shards), high / len(shards))
        return jnp.repeat(jnp.exp(draws), dims[axis_at] // blocks).reshape((-1,) + (1,) * (len(dims) - axis_at - 1))

    level = one(*shards[0])
    for cut in shards[1:]:
        level = level * one(*cut)
    return level


def assign_block(stream_key, own, number, rows, amount, top, most, skew):
    ranking = jax.random.permutation(stream_key, amount)
    packed, usual = shares(amount, rows * top, most, skew, True), shares(amount, rows * top, most, skew, False)
    places = jnp.arange(amount)

    def named(tallies, turn):
        used = int((tallies > 0).sum())
        fixed = max(1, used // 4)
        passed = fixed + (places - fixed + turn * (used - fixed)) % max(1, amount - fixed)
        return jnp.zeros((amount,), jnp.int32).at[ranking[jnp.where(places < fixed, places, passed)]].set(jnp.asarray(tallies, jnp.int32))

    tallies = jnp.where(number % 4 == 0, named(packed, number // 4), named(usual, number - number // 4 - 1))
    mixed = jax.random.permutation(jax.random.fold_in(own, 3), amount)
    source_of, taker = mixed[0:amount // 2 * 2:2], mixed[1:amount // 2 * 2:2]
    room = jnp.minimum(tallies[source_of] - 1, most - tallies[taker]) // 2
    room = jnp.where((source_of == ranking[0]) | (taker == ranking[0]) | (tallies[taker] == 0), 0, jnp.maximum(room, 0))
    passed = jax.random.randint(jax.random.fold_in(own, 4), (amount // 2,), 0, 1 << 20) % (room + 1)
    tallies = tallies.at[source_of].add(-passed).at[taker].add(passed)
    labels = jnp.searchsorted(jnp.cumsum(tallies), jnp.arange(rows * top), side="right").astype(jnp.int32)
    listing = labels.reshape(top, rows).T
    listing = listing[jax.random.permutation(jax.random.fold_in(own, 1), rows)]
    turn = jax.random.randint(jax.random.fold_in(own, 2), (rows, 1), 0, top)
    return jnp.take_along_axis(listing, (jnp.arange(top)[None, :] + turn) % top, axis=1)


def shares(count, total, limit, lean, full):
    weights = [(1 << 20) // math.isqrt(rank ** lean) + 1 for rank in range(1, count + 1)]
    largest = limit if full else min(limit, max(-(-total // count), total * weights[0] // sum(weights)))
    least = 1 if total - largest >= count - 1 else 0
    holding, rest = [largest] + [least] * (count - 1), total - largest - least * (count - 1)
    while rest > 0:
        movable = [i for i in range(1, count) if holding[i] < largest] or [i for i in range(1, count) if holding[i] < limit]
        mass, left = sum([weights[i] for i in movable]), rest
        for i in movable:
            extra = min(limit - holding[i], max(1, left * weights[i] // mass), rest)
            holding[i] = holding[i] + extra
            rest = rest - extra
    return np.array(holding)


def bell_draw(own_key, extent, scale, reach, cuts=(), kind=jnp.bfloat16):
    entries = jax.random.normal(own_key, extent, jnp.float32) * scale
    if len(cuts) > 0:
        entries = block_levels(own_key, extent, cuts, -0.22, 0.18) * entries
    return jnp.clip(entries, min=-reach, max=reach).astype(kind)


def setup_inputs(seed: int = 0, part: int = 0) -> dict:
    streams_of = jax.random.split(jax.random.key(seed), 8)
    part_keys = jax.random.split(jax.random.fold_in(streams_of[7], part), 8)
    exposure = draw_exposure(jax.random.fold_in(jax.random.fold_in(streams_of[7], part), 71), part)
    psf_taps = bell_draw(part_keys[1], (EXPOSURES, TAPS), 0.25, 1.5, ((0, 64),))
    col_warp = bell_draw(part_keys[2], (EXPOSURES * W, W), W ** -0.5, 0.25, ((0, 64),))
    row_warp = bell_draw(part_keys[3], (OUT_ROWS, R), R ** -0.5, 0.1875, ((0, 64),))
    row_patch_keys = jax.random.split(jax.random.fold_in(part_keys[4], 1), OUT_ROWS // RO)
    row_patch_turns = jax.random.permutation(jax.random.fold_in(part_keys[4], 3), OUT_ROWS // RO)
    row_patch = jax.vmap(lambda own, number: assign_block(jax.random.fold_in(part_keys[4], 2), own, number, RO, NPATCH, 1, CAP, 2))(row_patch_keys, row_patch_turns).reshape((OUT_ROWS, 1))
    row_prow = with_ends(jax.random.randint(part_keys[5], (OUT_ROWS,), 0, PATCH_ROWS), jax.random.fold_in(part_keys[5], 1), 0, PATCH_ROWS - 1).astype(jnp.int32)
    owner_map = jax.random.permutation(part_keys[6], NPATCH).astype(jnp.int32)
    return {"exposure": exposure, "psf_taps": psf_taps, "col_warp": col_warp, "row_warp": row_warp, "row_patch": row_patch, "row_prow": row_prow, "owner_map": owner_map}


def make_band(taps, width):
    half = (TAPS - 1) // 2
    rows_idx = jnp.arange(width, dtype=jnp.int32)[:, None]
    cols_idx = jnp.arange(width, dtype=jnp.int32)[None, :]
    offset = rows_idx - cols_idx + half
    band = jnp.zeros((width, width), jnp.bfloat16)
    for tap in range(TAPS):
        band = jnp.where(offset == tap, taps[tap], band)
    return band


def reference(exposure, psf_taps, col_warp, row_warp, row_patch, row_prow, owner_map):
    pieces = exposure.reshape(EXPOSURES, R, W)
    first = pieces[:, :STRIP]
    last = pieces[:, R - STRIP:]
    diff = last - jnp.roll(first, -1, axis=0)
    off_next = jnp.mean(diff.reshape(EXPOSURES, STRIP, W // 128, 128), axis=(1, 3))
    off_prev = jnp.roll(off_next, 1, axis=0)
    shift = jnp.repeat(-0.5 * off_next + 0.5 * off_prev, 128, axis=1)
    corrected = (pieces + shift[:, None, :]).astype(jnp.bfloat16)
    cw = col_warp.reshape(EXPOSURES, W, W)
    rw = row_warp.reshape(EXPOSURES, RO, R)

    def one_piece(items):
        image, taps, colw, roww = items
        band = make_band(taps, W)
        matched = jnp.dot(image, band, preferred_element_type=jnp.float32).astype(jnp.bfloat16)
        warped_cols = jnp.dot(matched, colw, preferred_element_type=jnp.float32).astype(jnp.bfloat16)
        return jnp.dot(roww, warped_cols, preferred_element_type=jnp.float32)

    warped = lax.map(one_piece, (corrected, psf_taps, cw, rw)).reshape(OUT_ROWS, W)
    slot_of = jnp.zeros((NPATCH,), jnp.int32).at[owner_map].set(jnp.arange(NPATCH, dtype=jnp.int32))
    key = slot_of[row_patch[:, 0]] * PATCH_ROWS + row_prow
    sums = jax.ops.segment_sum(warped, key, num_segments=NPATCH * PATCH_ROWS)
    counts = jax.ops.segment_sum(jnp.ones((OUT_ROWS,), jnp.float32), key, num_segments=NPATCH * PATCH_ROWS)
    return sums / jnp.maximum(counts, 1.0)[:, None]
```

```python
import functools

import jax
import jax.numpy as jnp
from jax import lax
from jax.experimental import pallas as pl
from jax.experimental.pallas import tpu as pltpu
from jax.sharding import PartitionSpec as P

F32, BF16, I32 = jnp.float32, jnp.bfloat16, jnp.int32
MESH = pl.DeviceIdType.MESH

STRIP = 16
TAPS = 15
PROWS = 32
CAP = 16
NX, NZ = 4, 16
W, R, RO = 512, 1024, 512
LANES = 128

NA = 2
NB = 2
RB = 1
BROWS = NX * PROWS // RB
ORDER = (
    ("b", 1), ("b", 2), ("x", 0), ("a0", 0), ("b", 3), ("a0", 1), ("b", 4), ("x", 1), ("a1", 0), ("a0", 2), ("a1", 1), ("b", 5),
    ("a0", 3), ("a1", 2), ("b", 6), ("a0", 4), ("a1", 3), ("b", 7), ("a0", 5), ("a1", 4), ("bx", 0), ("a0", 6), ("a1", 5),
    ("a0", 7), ("a1", 6), ("a1", 7),
)


def nt(a, b):
    return lax.dot_general(a, b, (((1,), (1,)), ((), ())), preferred_element_type=F32)


def mm(a, b):
    return jnp.dot(a, b, preferred_element_type=F32)


def iota(shape, dim):
    return lax.broadcasted_iota(I32, shape, dim)


def kernel(
    expo, taps, cw_hbm, rw_hbm, patch, prow, owner, out,
    ex, cw, rw, mat, tbuf, wbuf, sel, pack, halo_out, halo_in, cnt,
    bown, bring, bsend, brecv, xsend, xrecv, msend, mrecv, acc, aring,
    in_sem, hs, hr, bs, br, bxs, bxr, xs, xr, ms, mr, az, ar,
):
    e = lax.axis_index("exp")
    x, z = e // NZ, lax.rem(e, NZ)

    def dev(i):
        return {"exp": i}

    def at_z(d):
        return x * NZ + lax.rem(z + d + NZ, NZ)

    def at_x(d):
        return lax.rem(x + d + NX, NX) * NZ + z

    def remote(src, dst, s, r, target):
        return pltpu.make_async_remote_copy(
            src_ref=src, dst_ref=dst, send_sem=s, recv_sem=r, device_id=dev(target), device_id_type=MESH
        )

    nxt, prv = lax.rem(e + 1, NX * NZ), lax.rem(e + NX * NZ - 1, NX * NZ)

    quarter = R // 4
    loads = []
    for k, q in enumerate((0, 3, 1, 2)):
        rows = pl.ds(q * quarter, quarter)
        loads.append(pltpu.make_async_copy(expo.at[rows], ex.at[rows], in_sem.at[k]))
    loads.append(pltpu.make_async_copy(cw_hbm, cw, in_sem.at[4]))
    loads.append(pltpu.make_async_copy(rw_hbm, rw, in_sem.at[5]))
    for load in loads:
        load.start()

    barrier = pltpu.get_barrier_semaphore()
    peers = (at_z(1), at_z(-1), at_x(1), at_x(2), at_x(3), nxt, prv)
    for peer in peers:
        pl.semaphore_signal(barrier, inc=1, device_id=dev(peer), device_id_type=MESH)

    eye = iota((64, 64), 0) == iota((64, 64), 1)
    owner_col = jnp.sum(jnp.where(eye, jnp.broadcast_to(owner[...], (64, 64)), 0), axis=1, keepdims=True)
    own_of = owner_col == patch[...]
    slot_id = iota((64, RO), 0)
    dest = jnp.sum(jnp.where(own_of, slot_id, 0), axis=0, keepdims=True)
    dest_x, dest_z = dest // NZ, lax.rem(dest, NZ)
    in_z = dest_x * PROWS + prow[...]
    key = dest_z * (NX * PROWS) + in_z

    one_hot = jnp.where(own_of, 1.0, 0.0)
    before = jnp.where(iota((RO, RO), 0) < iota((RO, RO), 1), 1.0, 0.0).astype(BF16)
    earlier = mm(one_hot.astype(BF16), before)
    rank = jnp.sum(one_hot * earlier, axis=0, keepdims=True).astype(I32)
    slot = dest_x * (NZ * CAP) + dest_z * CAP + rank

    loads[0].wait()
    loads[1].wait()

    def means(rows):
        total = jnp.sum(ex[rows, :], axis=0, keepdims=True)
        parts = [
            jnp.broadcast_to(
                jnp.sum(total[:, b * LANES : (b + 1) * LANES], axis=1, keepdims=True) * (1.0 / (STRIP * LANES)), (1, LANES)
            )
            for b in range(W // LANES)
        ]
        return jnp.concatenate(parts, axis=1)

    first, last = means(slice(0, STRIP)), means(slice(R - STRIP, R))
    halo_out[0] = jnp.broadcast_to(first, (8, W))
    halo_out[1] = jnp.broadcast_to(last, (8, W))

    prow_row = jnp.broadcast_to((prow[...] + 1).astype(F32), (8, RO)).astype(BF16)
    for g in range(NX):
        place = jnp.where(iota((NZ * CAP, RO), 0) == slot - g * (NZ * CAP), 1.0, 0.0).astype(BF16)
        pack[g] = place
        msend[g] = nt(prow_row, place)

    pl.semaphore_wait(barrier, len(peers))
    halo = [
        remote(halo_out.at[0], halo_in.at[0], hs.at[0], hr.at[0], prv),
        remote(halo_out.at[1], halo_in.at[1], hs.at[1], hr.at[1], nxt),
    ]
    for copy in halo:
        copy.start()
    meta = []
    for k in (1, 2, 3):
        g = lax.rem(x + k, NX)
        meta.append(remote(msend.at[g], mrecv.at[k - 1], ms.at[k - 1], mr.at[k - 1], at_x(k)))
        meta[-1].start()

    oz = jnp.where(iota((NZ, RO), 0) == dest_z, 1.0, 0.0).astype(BF16)
    oq = jnp.where(iota((LANES, RO), 0) == in_z, 1.0, 0.0).astype(BF16)
    cnt[...] = nt(oz, oq)

    @pl.loop(0, NZ)
    def _(d):
        sel[pl.ds(pl.multiple_of(d * LANES, LANES), LANES), :] = jnp.where(
            iota((LANES, RO), 0) == key - d * LANES, 1.0, 0.0
        ).astype(BF16)

    offset = iota((LANES, 3 * LANES), 0) - iota((LANES, 3 * LANES), 1) + (LANES + (TAPS - 1) // 2)
    band = jnp.zeros((LANES, 3 * LANES), F32)
    tap = taps[...].astype(F32)
    for t in range(TAPS):
        band = jnp.where(offset == t, jnp.broadcast_to(tap[:, t : t + 1], (LANES, 3 * LANES)), band)
    band = band.astype(BF16)
    loads[4].wait()
    for b in range(W // LANES):
        low, high = max(b - 1, 0), min(b + 2, W // LANES)
        strip = band[:, (low - b + 1) * LANES : (high - b + 1) * LANES]
        mat[b * LANES : (b + 1) * LANES, :] = mm(strip, cw[low * LANES : high * LANES, :]).astype(BF16)

    loads[2].wait()
    loads[3].wait()
    loads[5].wait()
    for copy in halo:
        copy.wait_recv()
    off_next = last - halo_in[0][0:1]
    off_prev = halo_in[1][0:1] - first
    shift = -0.5 * off_next + 0.5 * off_prev

    @pl.loop(0, 4)
    def _(q):
        rows = pl.ds(pl.multiple_of(q * quarter, quarter), quarter)
        corrected = (ex[rows, :] + shift).astype(BF16)
        tbuf[rows, :] = mm(corrected, mat[...]).astype(BF16)

    @pl.loop(0, 2)
    def _(q):
        rows = pl.ds(pl.multiple_of(q * 256, 256), 256)
        wbuf[rows, :] = mm(rw[rows, :], tbuf[...]).astype(BF16)

    started = []

    def start(copy):
        copy.start()
        started.append(copy)

    def send_packed(c):
        cols = slice(c * LANES, (c + 1) * LANES)
        for k in (2, 1, 3, 0):
            g = lax.rem(x + k, NX)
            xsend[c, k] = mm(pack[g], wbuf[:, cols])
            if k:
                start(remote(xsend.at[c, k], xrecv.at[c, k - 1], xs.at[c, k - 1], xr.at[c, k - 1], at_x(k)))

    def place_of(packed_prow):
        spot = packed_prow.astype(I32)
        k = iota((1, NZ * CAP), 1) // CAP * PROWS + spot - 1
        k = jnp.where(spot > 0, k, -1)
        return jnp.where(iota((NZ * PROWS, NZ * CAP), 0) == k, 1.0, 0.0).astype(BF16)

    spread = []

    def take_packed(c):
        if not spread:
            spread.append(place_of(msend[x][0:1]))
            for k in (1, 2, 3):
                remote(msend.at[0], mrecv.at[k - 1], ms.at[k - 1], mr.at[k - 1], at_x(k)).wait_recv()
                spread.append(place_of(mrecv[k - 1][0:1]))
        total = mm(spread[0], xsend[c, 0].astype(BF16))
        for k in (1, 3, 2):
            remote(xsend.at[c, k], xrecv.at[c, k - 1], xs.at[c, k - 1], xr.at[c, k - 1], at_x(k)).wait_recv()
            total += mm(spread[k], xrecv[c, k - 1].astype(BF16))
        acc[c] = total

    def hops(direction, unit):
        return NZ // 2 if (unit + direction) % 2 == 0 else NZ // 2 - 1

    def ring_dest(direction, unit, step):
        left = hops(direction, unit) - step
        return lax.rem(z + (left if direction == 0 else -left) + NZ, NZ)

    def b_value(c, part, d):
        rows = pl.ds(pl.multiple_of(d * LANES + part * BROWS, BROWS), BROWS)
        return mm(sel[rows, :], wbuf[:, (NA + c) * LANES : (NA + c + 1) * LANES])

    def counts_of(d):
        return jnp.broadcast_to(cnt[pl.ds(d, 1), :], (8, LANES))

    def b_rows(u):
        return BROWS + 8 if u == 0 else BROWS

    def b_copy(direction, u, step):
        rows = pl.ds(0, b_rows(u))
        source = bown.at[direction, u, rows] if step == 0 else bring.at[direction, step - 1, u, rows]
        return remote(
            source,
            bring.at[direction, step, u, rows],
            bs.at[direction, step, u],
            br.at[direction, step, u],
            at_z(1 if direction == 0 else -1),
        )

    def b_step(step):
        for u in range(NB * RB):
            c, part = u // RB, u % RB
            for direction in (0, 1):
                if step >= hops(direction, u):
                    continue
                d = ring_dest(direction, u, step)
                value = b_value(c, part, d)
                if step == 0:
                    bown[direction, u, 0:BROWS] = value
                    if u == 0:
                        bown[direction, u, BROWS : BROWS + 8] = counts_of(d)
                else:
                    b_copy(direction, u, step - 1).wait_recv()
                    bring[direction, step - 1, u, 0:BROWS] += value
                    if u == 0:
                        bring[direction, step - 1, u, BROWS : BROWS + 8] += counts_of(d)
                start(b_copy(direction, u, step))

    def b_last():
        for u in range(NB * RB):
            c, part = u // RB, u % RB
            cols = slice(c * LANES, (c + 1) * LANES)
            value = b_value(c, part, z)
            number = counts_of(z)
            for direction in (0, 1):
                step = hops(direction, u) - 1
                b_copy(direction, u, step).wait_recv()
                value += bring[direction, step, u, 0:BROWS]
                if u == 0:
                    number += bring[direction, step, u, BROWS : BROWS + 8]
            for g in range(BROWS // PROWS):
                bsend[part * (BROWS // PROWS) + g, 0:PROWS, cols] = value[g * PROWS : (g + 1) * PROWS]
            if u == 0:
                for g in range(NX):
                    bsend[g, PROWS : PROWS + 8, 0:LANES] = number
                    for other in range(1, NB):
                        bsend[g, PROWS : PROWS + 8, other * LANES : (other + 1) * LANES] = number
        for k in (2, 1, 3):
            start(remote(bsend.at[lax.rem(x + k, NX)], brecv.at[k - 1], bxs.at[k - 1], bxr.at[k - 1], at_x(k)))

    def a_copy(direction, c, step):
        return remote(
            acc.at[c, pl.ds(pl.multiple_of(ring_dest(direction, c, 0) * PROWS, PROWS), PROWS)]
            if step == 0
            else aring.at[direction, step - 1, c],
            aring.at[direction, step, c],
            az.at[direction, step, c],
            ar.at[direction, step, c],
            at_z(1 if direction == 0 else -1),
        )

    def a_step(c, step):
        for direction in (0, 1):
            if step >= hops(direction, c):
                continue
            if step:
                d = ring_dest(direction, c, step)
                a_copy(direction, c, step - 1).wait_recv()
                aring[direction, step - 1, c] += acc[c, pl.ds(pl.multiple_of(d * PROWS, PROWS), PROWS), :]
            start(a_copy(direction, c, step))

    b_step(0)
    for c in range(NA):
        send_packed(c)
    for what, step in ORDER:
        if what == "b":
            b_step(step)
        elif what == "x":
            take_packed(step)
        elif what == "bx":
            b_last()
        else:
            a_step(int(what[1]), step)

    for k in (1, 3, 2):
        remote(bsend.at[0], brecv.at[k - 1], bxs.at[k - 1], bxr.at[k - 1], at_x(k)).wait_recv()
    total = bsend[x] + brecv[0] + brecv[1] + brecv[2]
    here = iota((PROWS, LANES), 1) == x * PROWS + iota((PROWS, LANES), 0)
    number = jnp.sum(jnp.where(here, jnp.broadcast_to(total[PROWS : PROWS + 1, 0:LANES], (PROWS, LANES)), 0.0), axis=1, keepdims=True)
    number = jnp.maximum(number, 1.0)
    out[:, NA * LANES :] = total[0:PROWS] / number
    for c in range(NA):
        value = acc[c, pl.ds(pl.multiple_of(z * PROWS, PROWS), PROWS), :]
        for direction in (0, 1):
            step = hops(direction, c) - 1
            a_copy(direction, c, step).wait_recv()
            value += aring[direction, step, c]
        out[:, c * LANES : (c + 1) * LANES] = value / number

    for copy in halo + meta + started:
        copy.wait_send()


def on_device(exposure, psf_taps, col_warp, row_warp, row_patch, row_prow, owner_map):
    vmem = pl.BlockSpec(memory_space=pltpu.VMEM)
    anywhere = pl.BlockSpec(memory_space=pl.ANY)
    steps = NZ // 2
    dma = pltpu.SemaphoreType.DMA
    return pl.pallas_call(
        kernel,
        out_shape=jax.ShapeDtypeStruct((PROWS, W), F32),
        in_specs=[anywhere, vmem, anywhere, anywhere, vmem, vmem, vmem],
        out_specs=vmem,
        scratch_shapes=[
            pltpu.VMEM((R, W), F32),
            pltpu.VMEM((W, W), BF16),
            pltpu.VMEM((RO, R), BF16),
            pltpu.VMEM((W, W), BF16),
            pltpu.VMEM((R, W), BF16),
            pltpu.VMEM((RO, W), BF16),
            pltpu.VMEM((NX * NZ * PROWS, RO), BF16),
            pltpu.VMEM((NX, NZ * CAP, RO), BF16),
            pltpu.VMEM((2, 8, W), F32),
            pltpu.VMEM((2, 8, W), F32),
            pltpu.VMEM((NZ, LANES), F32),
            pltpu.VMEM((2, NB * RB, BROWS + 8, LANES), F32),
            pltpu.VMEM((2, steps, NB * RB, BROWS + 8, LANES), F32),
            pltpu.VMEM((NX, PROWS + 8, NB * LANES), F32),
            pltpu.VMEM((NX - 1, PROWS + 8, NB * LANES), F32),
            pltpu.VMEM((NA, NX, NZ * CAP, LANES), F32),
            pltpu.VMEM((NA, NX - 1, NZ * CAP, LANES), F32),
            pltpu.VMEM((NX, 8, NZ * CAP), F32),
            pltpu.VMEM((NX - 1, 8, NZ * CAP), F32),
            pltpu.VMEM((NA, NZ * PROWS, LANES), F32),
            pltpu.VMEM((2, steps, NA, PROWS, LANES), F32),
            dma((6,)),
            dma((2,)),
            dma((2,)),
            dma((2, steps, NB * RB)),
            dma((2, steps, NB * RB)),
            dma((NX - 1,)),
            dma((NX - 1,)),
            dma((NA, NX - 1)),
            dma((NA, NX - 1)),
            dma((NX - 1,)),
            dma((NX - 1,)),
            dma((2, steps, NA)),
            dma((2, steps, NA)),
        ],
        compiler_params=pltpu.CompilerParams(collective_id=0, has_side_effects=True),
    )(
        exposure,
        psf_taps,
        col_warp,
        row_warp,
        row_patch.reshape(1, RO),
        row_prow.reshape(1, RO),
        owner_map.reshape(1, -1),
    )


def solution(mesh):
    placed = (
        P(("band", "exp"), None),
        P(("band", "exp"), None),
        P(("band", "exp"), None),
        P(("band", "exp"), None),
        P(("band", "exp"), None),
        P(("band", "exp")),
        P("band"),
    )
    return jax.shard_map(
        on_device, mesh=mesh, in_specs=placed, out_specs=P(("band", "exp"), None), check_vma=False
    )
```

```python
import functools

import jax
import jax.numpy as jnp
from jax import lax
from jax.experimental import pallas as pl
from jax.experimental.pallas import tpu as pltpu
from jax.sharding import PartitionSpec as P

F32, BF16, I32 = jnp.float32, jnp.bfloat16, jnp.int32
MESH = pl.DeviceIdType.MESH

STRIP = 16
TAPS = 15
PROWS = 32
CAP = 16
NX, NZ = 4, 16
W, R, RO = 512, 1024, 512
LANES = 128

NC = W // LANES
OWN, OPP = 0, 1
NM = NZ - 1
SIDES = (1, 3)

UNITS = (
    (OWN, 0, 256, 40),
    (OWN, 256, 256, 32),
    (OPP, 0, 128, 40),
    (OPP, 128, 128, 32),
    (OPP, 256, 128, 32),
    (OPP, 384, 128, 32),
)
NOWN = sum(u[0] == OWN for u in UNITS)
GROUPS = ((0, 2), (2, 4), (4, 8), (8, 12), (12, 16))
ORDER = (
    (2, 0, 1), (2, 1, 1), (3, 1, 1), (3, 0, 1), ("x", 0), (4, 0, 1), (4, 1, 1), (0, 0, 0), (5, 1, 1), (5, 0, 1),
    (1, 1, 0), (0, 1, 0), ("x", 1), (2, 0, 2), (2, 1, 2), (1, 0, 0), (3, 0, 2), (3, 1, 2), (4, 0, 2), (4, 1, 2),
    (5, 1, 2), (0, 0, 1), (1, 1, 1), (5, 0, 2), (2, 0, 3), ("x", 2), (0, 1, 1), (1, 0, 1), (2, 1, 3), (3, 0, 3),
    (3, 1, 3), (4, 0, 3), (4, 1, 3), (5, 1, 3), (0, 0, 2), (1, 1, 2), (5, 0, 3), ("x", 3), (2, 0, 4), (0, 1, 2),
    (1, 0, 2), (2, 1, 4), (3, 0, 4), (3, 1, 4), (4, 0, 4), (4, 1, 4), (5, 1, 4), (0, 0, 3), (1, 1, 3), (5, 0, 4),
    ("x", 4), (2, 0, 5), (0, 1, 3), (1, 0, 3), (2, 1, 5), (3, 0, 5), (3, 1, 5), (4, 0, 5), (4, 1, 5), (5, 1, 5),
    (0, 0, 4), (1, 1, 4), (5, 0, 5), (2, 0, 6), (0, 1, 4), (1, 0, 4), (2, 1, 6), (3, 0, 6), (3, 1, 6), (4, 0, 6),
    (4, 1, 6), (5, 1, 6), (0, 0, 5), (1, 1, 5), (5, 0, 6), (2, 0, 7), (0, 1, 5), (1, 0, 5), (3, 1, 7), (4, 0, 7),
    (5, 1, 7), (0, 0, 6), (1, 1, 6), ("o", 2), (0, 1, 6), ("o", 3), (1, 0, 6), ("o", 5), ("o", 4), (0, 0, 7),
    (1, 1, 7),
)


def far(n, direction):
    return NZ // 2 if (n + direction) % 2 == 0 else NZ // 2 - 1


def spot_of(n, direction, step):
    left = far(n, direction) - step
    away = left if direction == 0 else NZ - left
    return 2 * (NZ // 2 - away) if away <= NZ // 2 else 2 * (away - NZ // 2 - 1) + 1


def nt(a, b):
    return lax.dot_general(a, b, (((1,), (1,)), ((), ())), preferred_element_type=F32)


def mm(a, b):
    return jnp.dot(a, b, preferred_element_type=F32)


def iota(shape, dim):
    return lax.broadcasted_iota(I32, shape, dim)


def equal(a, b):
    return jnp.where(a == b, 1.0, 0.0).astype(BF16)


def kernel(
    expo, taps_hbm, cw_hbm, rw_hbm, patch_hbm, prow_hbm, owner_hbm, out,
    ex, strips, taps, cw, rw, patch, prow, owner, mat, corr, ybuf, wbuf, sel, pack, halo_out, halo_in,
    msend, mrecv, in_sem, hs, hr, ms, mr, xs, xr, rs, rr, os, oR, *buffers,
):
    buffers = list(buffers)

    def take(number):
        return [buffers.pop(0) for _ in range(number)]

    count = len(UNITS)
    acc, ring, osend, orecv = take(count), take(count), take(count - NOWN), take(count - NOWN)
    xsend, xrecv, place = take(len(GROUPS)), take(len(GROUPS)), take(len(GROUPS))
    e = lax.axis_index("exp")
    x, z = e // NZ, lax.rem(e, NZ)

    def dev(i):
        return {"exp": i}

    def at_z(d):
        return x * NZ + lax.rem(z + d + NZ, NZ)

    def at_x(d):
        return lax.rem(x + d + NX, NX) * NZ + z

    def remote(src, dst, s, r, target):
        return pltpu.make_async_remote_copy(
            src_ref=src, dst_ref=dst, send_sem=s, recv_sem=r, device_id=dev(target), device_id_type=MESH
        )

    nxt, prv = lax.rem(e + 1, NX * NZ), lax.rem(e + NX * NZ - 1, NX * NZ)

    loads = []

    def load(src, dst):
        copy = pltpu.make_async_copy(src, dst, in_sem.at[len(loads)])
        copy.start()
        loads.append(copy)
        return copy

    strip_loads = [load(expo.at[pl.ds(0, STRIP)], strips.at[0]), load(expo.at[pl.ds(R - STRIP, STRIP)], strips.at[1])]
    barrier = pltpu.get_barrier_semaphore()
    peers = [nxt, prv, at_z(1), at_z(-1), at_x(1), at_x(3), at_x(2)]
    for peer in peers:
        pl.semaphore_signal(barrier, inc=1, device_id=dev(peer), device_id_type=MESH)
    key_loads = [load(owner_hbm, owner), load(patch_hbm, patch), load(prow_hbm, prow)]
    piece_load = load(expo, ex)
    row_load = load(rw_hbm, rw)
    mat_loads = [load(taps_hbm, taps), load(cw_hbm, cw)]

    for copy in strip_loads:
        copy.wait()

    def means(strip):
        total = jnp.sum(strip, axis=0, keepdims=True)
        parts = [
            jnp.broadcast_to(
                jnp.sum(total[:, b * LANES : (b + 1) * LANES], axis=1, keepdims=True) * (1.0 / (STRIP * LANES)), (1, LANES)
            )
            for b in range(NC)
        ]
        return jnp.concatenate(parts, axis=1)

    first, last = means(strips[0]), means(strips[1])
    halo_out[0] = jnp.broadcast_to(first, (8, W))
    halo_out[1] = jnp.broadcast_to(last, (8, W))
    pl.semaphore_wait(barrier, len(peers))
    halo = [
        remote(halo_out.at[0], halo_in.at[0], hs, hr.at[0], prv),
        remote(halo_out.at[1], halo_in.at[1], hs, hr.at[1], nxt),
    ]
    for copy in halo:
        copy.start()

    for copy in key_loads:
        copy.wait()
    eye = iota((NX * NZ, NX * NZ), 0) == iota((NX * NZ, NX * NZ), 1)
    owner_col = jnp.sum(jnp.where(eye, jnp.broadcast_to(owner[...], eye.shape), 0), axis=1, keepdims=True)
    own_of = owner_col == patch[...]
    dest = jnp.sum(jnp.where(own_of, iota((NX * NZ, RO), 0), 0), axis=0, keepdims=True)
    dest_x, dest_z = dest // NZ, lax.rem(dest, NZ)
    one_hot = jnp.where(own_of, 1.0, 0.0)
    before = jnp.where(iota((RO, RO), 0) < iota((RO, RO), 1), 1.0, 0.0).astype(BF16)
    earlier = mm(one_hot.astype(BF16), before)
    rank = jnp.sum(one_hot * earlier, axis=0, keepdims=True).astype(I32)
    away = lax.rem(dest_z - z + NZ, NZ)
    near = NZ // 2
    spot = jnp.where(away == 0, NZ - 1, jnp.where(away <= near, 2 * (near - away), 2 * (away - near) - 1))
    slot = spot * CAP + rank

    prow_row = jnp.broadcast_to((prow[...] + 1).astype(F32), (8, RO)).astype(BF16)
    meta = []
    for i, k in enumerate(SIDES):
        to = dest_x == lax.rem(x + k, NX)
        pack[i] = equal(iota((NZ * CAP, RO), 0), jnp.where(to, slot, -1))
        msend[i] = nt(prow_row, pack[i])
        meta.append(remote(msend.at[i], mrecv.at[i], ms, mr.at[i], at_x(k)))
        meta[-1].start()

    oz = equal(iota((NZ, RO), 0), spot)
    counts = []
    for kind in (OWN, OPP):
        to = dest_x == lax.rem(x + 2 * kind, NX)
        key = jnp.where(to, spot * PROWS + prow[...], -1)
        sel[kind] = equal(iota((NZ * PROWS, RO), 0), key)
        counts.append(nt(oz, equal(iota((LANES, RO), 0), jnp.where(to, prow[...], -1))))

    offset = iota((LANES, 3 * LANES), 0) - iota((LANES, 3 * LANES), 1) + (LANES + (TAPS - 1) // 2)
    for copy in mat_loads:
        copy.wait()
    band = jnp.zeros((LANES, 3 * LANES), F32)
    tap = taps[...].astype(F32)
    for t in range(TAPS):
        band = jnp.where(offset == t, jnp.broadcast_to(tap[:, t : t + 1], (LANES, 3 * LANES)), band)
    band = band.astype(BF16)
    for b in range(NC):
        low, high = max(b - 1, 0), min(b + 2, NC)
        strip = band[:, (low - b + 1) * LANES : (high - b + 1) * LANES]
        mat[b * LANES : (b + 1) * LANES, :] = mm(strip, cw[low * LANES : high * LANES, :]).astype(BF16)

    piece_load.wait()
    row_load.wait()
    for copy in halo:
        copy.wait_recv()
    off_next = last - halo_in[0][0:1]
    off_prev = halo_in[1][0:1] - first
    shift = -0.5 * off_next + 0.5 * off_prev

    def x_copy(g, i):
        return remote(xsend[g].at[i], xrecv[g].at[i], xs.at[g], xr.at[g, i], at_x(SIDES[i]))

    def chain_copy(n, direction, step):
        m = step if direction == 0 else far(n, 0) + step
        source = ring[n].at[m - 1] if step else acc[n].at[spot_of(n, direction, 0)]
        return remote(source, ring[n].at[m], rs.at[n], rr.at[n, m], at_z(1 if direction == 0 else -1))

    def chain_step(n, direction, step):
        if step:
            m = step if direction == 0 else far(n, 0) + step
            chain_copy(n, direction, step - 1).wait_recv()
            ring[n][m - 1] += acc[n][spot_of(n, direction, step)]
        chain_copy(n, direction, step).start()

    def chain_total(n):
        total = acc[n][NZ - 1]
        for direction in (0, 1):
            step = far(n, direction) - 1
            chain_copy(n, direction, step).wait_recv()
            total += ring[n][step if direction == 0 else far(n, 0) + step]
        return total

    def opp_copy(n):
        return remote(osend[n - NOWN], orecv[n - NOWN], os.at[n - NOWN], oR.at[n - NOWN], at_x(2))

    def opp_last(n):
        osend[n - NOWN][...] = chain_total(n)
        opp_copy(n).start()

    def spread(packed, i):
        at = packed[0:1].astype(I32)
        lane = iota((1, NZ * CAP), 1) // CAP
        key = jnp.where(at > 0, lane * PROWS + at - 1, -1)
        for g, (low, high) in enumerate(GROUPS):
            part = key[:, low * CAP : high * CAP]
            place[g][i] = equal(iota(((high - low) * PROWS, (high - low) * CAP), 0) + low * PROWS, part)
        return nt(equal(iota((NZ, NZ * CAP), 0), lane), equal(iota((LANES, NZ * CAP), 0), at - 1))

    def columns(n):
        return slice(UNITS[n][1], UNITS[n][1] + UNITS[n][2])

    def take_packed(g):
        low, high = GROUPS[g]
        for i in (0, 1):
            x_copy(g, i).wait_recv()
        for n in range(NOWN):
            shape = (high - low, PROWS, UNITS[n][2])
            total = acc[n][low:high, 0:PROWS].reshape(shape[0] * PROWS, shape[2])
            for i in (0, 1):
                total += mm(place[g][i], xrecv[g][i, :, columns(n)].astype(BF16))
            acc[n][low:high, 0:PROWS] = total.reshape(shape)

    def fill_counts(n, number):
        tile = jnp.broadcast_to(number[:, None, :], (NZ, 8, LANES))
        for part in range(UNITS[n][2] // LANES):
            acc[n][:, PROWS:, part * LANES : (part + 1) * LANES] = tile

    def send_packed(g):
        low, high = GROUPS[g]
        for i in (0, 1):
            xsend[g][i] = mm(pack[i, low * CAP : high * CAP], wbuf[...])
            x_copy(g, i).start()

    def dense(n):
        acc[n][:, 0:PROWS] = mm(sel[UNITS[n][0]], wbuf[:, columns(n)]).reshape(NZ, PROWS, UNITS[n][2])

    fill_counts(NOWN, counts[OPP])

    corr[...] = (ex[...] + shift).astype(BF16)
    ybuf[...] = mm(rw[...], corr[...]).astype(BF16)
    wbuf[...] = mm(ybuf[...], mat[...]).astype(BF16)
    send_packed(0)
    for n in range(NOWN, count):
        dense(n)
        for direction in (0, 1):
            chain_step(n, direction, 0)
    for g in range(1, len(GROUPS)):
        send_packed(g)
    for n in range(NOWN):
        dense(n)

    number = counts[OWN]
    for i in (0, 1):
        meta[i].wait_recv()
        number += spread(mrecv[i], i)
    fill_counts(0, number)

    for step in ORDER:
        if step[0] == "x":
            take_packed(step[1])
        elif step[0] == "o":
            opp_last(step[1])
        else:
            chain_step(*step)

    diag = iota((PROWS, LANES), 1) == iota((PROWS, LANES), 0)
    for n in range(NOWN, count):
        opp_copy(n).wait_recv()
    for n in range(NOWN):
        total = chain_total(n)
        if n == 0:
            number = jnp.broadcast_to(total[PROWS : PROWS + 1, 0:LANES] + orecv[0][PROWS : PROWS + 1, 0:LANES], (PROWS, LANES))
            number = jnp.maximum(jnp.sum(jnp.where(diag, number, 0.0), axis=1, keepdims=True), 1.0)
        for c in range(UNITS[n][2] // LANES):
            first_column = UNITS[n][1] + c * LANES
            o = next(o for o in range(NOWN, count) if UNITS[o][1] <= first_column < UNITS[o][1] + UNITS[o][2])
            other = orecv[o - NOWN][0:PROWS, first_column - UNITS[o][1] : first_column - UNITS[o][1] + LANES]
            out[:, first_column : first_column + LANES] = (total[0:PROWS, c * LANES : (c + 1) * LANES] + other) / number

    remote(halo_out, halo_in, hs, hr.at[0], prv).wait_send()
    remote(msend, mrecv, ms, mr.at[0], at_x(1)).wait_send()
    for g in range(len(GROUPS)):
        remote(xsend[g], xrecv[g], xs.at[g], xr.at[g, 0], at_x(1)).wait_send()
    for n in range(count):
        remote(ring[n], ring[n], rs.at[n], rr.at[n, 0], at_z(1)).wait_send()
    for n in range(NOWN, count):
        opp_copy(n).wait_send()


def on_device(exposure, psf_taps, col_warp, row_warp, row_patch, row_prow, owner_map):
    anywhere = pl.BlockSpec(memory_space=pl.ANY)
    dma = pltpu.SemaphoreType.DMA
    vmem = pltpu.VMEM
    blocks = [(rows, width) for _, _, width, rows in UNITS]
    packs = [vmem((2, (high - low) * CAP, W), F32) for low, high in GROUPS]
    places = [vmem((2, (high - low) * PROWS, (high - low) * CAP), BF16) for low, high in GROUPS]
    others = [vmem(block, F32) for block in blocks[NOWN:]]
    return pl.pallas_call(
        kernel,
        out_shape=vmem((PROWS, W), F32),
        in_specs=[anywhere] * 7,
        out_specs=pl.BlockSpec(memory_space=vmem),
        scratch_shapes=[
            vmem((R, W), F32),
            vmem((2, STRIP, W), F32),
            vmem((1, TAPS), BF16),
            vmem((W, W), BF16),
            vmem((RO, R), BF16),
            vmem((1, RO), I32),
            vmem((1, RO), I32),
            vmem((1, NX * NZ), I32),
            vmem((W, W), BF16),
            vmem((R, W), BF16),
            vmem((RO, W), BF16),
            vmem((RO, W), BF16),
            vmem((2, NZ * PROWS, RO), BF16),
            vmem((2, NZ * CAP, RO), BF16),
            vmem((2, 8, W), F32),
            vmem((2, 8, W), F32),
            vmem((2, 8, NZ * CAP), F32),
            vmem((2, 8, NZ * CAP), F32),
            dma((9,)),
            dma(()),
            dma((2,)),
            dma(()),
            dma((2,)),
            dma((len(GROUPS),)),
            dma((len(GROUPS), 2)),
            dma((len(UNITS),)),
            dma((len(UNITS), NM)),
            dma((len(UNITS) - NOWN,)),
            dma((len(UNITS) - NOWN,)),
        ]
        + [vmem((NZ, *block), F32) for block in blocks]
        + [vmem((NM, *block), F32) for block in blocks]
        + others
        + others
        + packs
        + packs
        + places,
        compiler_params=pltpu.CompilerParams(collective_id=0, has_side_effects=True),
    )(
        exposure,
        psf_taps,
        col_warp,
        row_warp,
        row_patch.reshape(1, RO),
        row_prow.reshape(1, RO),
        owner_map.reshape(1, -1),
    )


def solution(mesh):
    placed = (
        P(("band", "exp"), None),
        P(("band", "exp"), None),
        P(("band", "exp"), None),
        P(("band", "exp"), None),
        P(("band", "exp"), None),
        P(("band", "exp")),
        P("band"),
    )
    return jax.shard_map(
        on_device, mesh=mesh, in_specs=placed, out_specs=P(("band", "exp"), None), check_vma=False
    )
```

```python
import functools

import jax
import jax.numpy as jnp
from jax import lax
from jax.experimental import pallas as pl
from jax.experimental.pallas import tpu as pltpu
from jax.sharding import PartitionSpec as P

F32, BF16, I32 = jnp.float32, jnp.bfloat16, jnp.int32
MESH = pl.DeviceIdType.MESH

STRIP = 16
TAPS = 15
PROWS = 32
CAP = 16
NX, NZ = 4, 16
W, R, RO = 512, 1024, 512
LANES = 128

NC = W // LANES
OWN, OPP = 0, 1
NM = NZ - 1
SIDES = (1, 3, 2)

UNITS = (
    (OWN, 0, 128, 33),
    (OWN, 128, 128, 32),
    (OWN, 256, 128, 32),
    (OWN, 384, 128, 32),
    (OPP, 0, 128, 33),
    (OPP, 128, 128, 32),
)
NOWN = sum(u[0] == OWN for u in UNITS)
ZFIRST = 256
NEAR = (2, 2)
SPOT = (15, 13, 11, 9, 7, 5, 3, 1, 0, 2, 4, 6, 8, 10, 12, 14)
GROUPS = ((0, 2), (2, 4), (4, 6), (6, 8), (8, 10), (10, 12), (12, 14), (14, 16))
ORDER = (
    (4, 0, 1), (4, 2, 1), (4, 1, 1), (4, 3, 1), (5, 2, 1), (5, 0, 1), (5, 1, 1), (5, 3, 1), ("x", 0), (0, 0, 0),
    (1, 2, 0), (2, 0, 0), (3, 2, 0), (1, 0, 0), (3, 0, 0), (4, 0, 2), (4, 2, 2), ("x", 1), (0, 2, 0), (2, 2, 0),
    (5, 0, 2), (5, 2, 2), (1, 2, 1), (0, 0, 1), (3, 2, 1), (2, 0, 1), (1, 0, 1), ("x", 2), (3, 0, 1), (4, 0, 3),
    (4, 2, 3), (0, 2, 1), (5, 0, 3), (2, 2, 1), (5, 2, 3), ("x", 3), (1, 2, 2), (0, 0, 2), (3, 2, 2), (2, 0, 2),
    (1, 0, 2), (3, 0, 2), (4, 0, 4), (4, 2, 4), ("x", 4), (0, 2, 2), (5, 0, 4), (2, 2, 2), (5, 2, 4), (1, 2, 3),
    (0, 0, 3), (3, 2, 3), (2, 0, 3), (1, 0, 3), ("x", 5), (0, 1, 0), (1, 1, 0), (2, 1, 0), (3, 1, 0), (3, 0, 3),
    (4, 0, 5), (0, 2, 3), (2, 2, 3), ("x", 6), (0, 3, 0), (1, 3, 0), (2, 3, 0), (3, 3, 0), (0, 0, 4), (5, 2, 5),
    (2, 0, 4), (1, 2, 4), (1, 0, 4), (3, 2, 4), (0, 1, 1), (1, 1, 1), (2, 1, 1), ("x", 7), (3, 1, 1), (3, 0, 4),
    (0, 2, 4), (2, 2, 4), (0, 3, 1), (1, 3, 1), (0, 0, 5), (2, 3, 1), (2, 0, 5), (3, 3, 1), ("o", 4), (1, 2, 5),
    (3, 2, 5), ("o", 5),
)


def chains(n):
    out, m, near = [], 0, NEAR[UNITS[n][0]]
    for direction in (0, 1):
        far = NZ // 2 if (n + direction) % 2 == 0 else NZ // 2 - 1
        for top, bottom in ((far, near), (near, 0)) if near else ((far, 0),):
            left = (*range(top, bottom, -1), 0)
            out.append((direction, left, m))
            m += len(left) - 1
    return out


def spot_of(chain, step):
    direction, left, _ = chain
    return SPOT[left[step] if direction == 0 else NZ - left[step]]


def nt(a, b):
    return lax.dot_general(a, b, (((1,), (1,)), ((), ())), preferred_element_type=F32)


def mm(a, b):
    return jnp.dot(a, b, preferred_element_type=F32)


def iota(shape, dim):
    return lax.broadcasted_iota(I32, shape, dim)


def equal(a, b):
    return jnp.where(a == b, 1.0, 0.0).astype(BF16)


def kernel(
    expo, taps_hbm, cw_hbm, rw_hbm, patch_hbm, prow_hbm, owner_hbm, out,
    ex, strips, taps, cw, rw, patch, prow, owner, mat, corr, ybuf, wbuf, sel, pack, halo_out, halo_in,
    msend, mrecv, in_sem, hs, hr, ms, mr, xs, ys, xr, rs, rr, os, oR, *buffers,
):
    buffers = list(buffers)

    def take(number):
        return [buffers.pop(0) for _ in range(number)]

    count = len(UNITS)
    acc, ring, osend, orecv = take(count), take(count), take(count - NOWN), take(count - NOWN)
    xsend, xrecv, place = take(len(GROUPS)), take(len(GROUPS)), take(len(GROUPS))
    ysend, yrecv = take(len(GROUPS)), take(len(GROUPS))
    e = lax.axis_index("exp")
    x, z = e // NZ, lax.rem(e, NZ)

    def dev(i):
        return {"exp": i}

    def at_z(d):
        return x * NZ + lax.rem(z + d + NZ, NZ)

    def at_x(d):
        return lax.rem(x + d + NX, NX) * NZ + z

    def remote(src, dst, s, r, target):
        return pltpu.make_async_remote_copy(
            src_ref=src, dst_ref=dst, send_sem=s, recv_sem=r, device_id=dev(target), device_id_type=MESH
        )

    nxt, prv = lax.rem(e + 1, NX * NZ), lax.rem(e + NX * NZ - 1, NX * NZ)

    loads = []

    def load(src, dst):
        copy = pltpu.make_async_copy(src, dst, in_sem.at[len(loads)])
        copy.start()
        loads.append(copy)
        return copy

    strip_loads = [load(expo.at[pl.ds(0, STRIP)], strips.at[0]), load(expo.at[pl.ds(R - STRIP, STRIP)], strips.at[1])]
    barrier = pltpu.get_barrier_semaphore()
    peers = [nxt, prv, at_z(1), at_z(-1), at_x(1), at_x(3), at_x(2)]
    for hop in sorted({near + 1 for near in NEAR if near}):
        peers += [at_z(hop), at_z(-hop)]
    for peer in peers:
        pl.semaphore_signal(barrier, inc=1, device_id=dev(peer), device_id_type=MESH)
    key_loads = [load(owner_hbm, owner), load(patch_hbm, patch), load(prow_hbm, prow)]
    piece_load = load(expo, ex)
    row_load = load(rw_hbm, rw)
    mat_loads = [load(taps_hbm, taps), load(cw_hbm, cw)]

    for copy in strip_loads:
        copy.wait()

    def means(strip):
        total = jnp.sum(strip, axis=0, keepdims=True)
        parts = [
            jnp.broadcast_to(
                jnp.sum(total[:, b * LANES : (b + 1) * LANES], axis=1, keepdims=True) * (1.0 / (STRIP * LANES)), (1, LANES)
            )
            for b in range(NC)
        ]
        return jnp.concatenate(parts, axis=1)

    first, last = means(strips[0]), means(strips[1])
    halo_out[0] = jnp.broadcast_to(first, (8, W))
    halo_out[1] = jnp.broadcast_to(last, (8, W))
    pl.semaphore_wait(barrier, len(peers))
    halo = [
        remote(halo_out.at[0], halo_in.at[0], hs, hr.at[0], prv),
        remote(halo_out.at[1], halo_in.at[1], hs, hr.at[1], nxt),
    ]
    for copy in halo:
        copy.start()

    for copy in key_loads:
        copy.wait()
    eye = iota((NX * NZ, NX * NZ), 0) == iota((NX * NZ, NX * NZ), 1)
    owner_col = jnp.sum(jnp.where(eye, jnp.broadcast_to(owner[...], eye.shape), 0), axis=1, keepdims=True)
    own_of = owner_col == patch[...]
    dest = jnp.sum(jnp.where(own_of, iota((NX * NZ, RO), 0), 0), axis=0, keepdims=True)
    dest_x, dest_z = dest // NZ, lax.rem(dest, NZ)
    one_hot = jnp.where(own_of, 1.0, 0.0)
    before = jnp.where(iota((RO, RO), 0) < iota((RO, RO), 1), 1.0, 0.0).astype(BF16)
    earlier = mm(one_hot.astype(BF16), before)
    rank = jnp.sum(one_hot * earlier, axis=0, keepdims=True).astype(I32)
    away = lax.rem(dest_z - z + NZ, NZ)
    spot = sum(jnp.where(away == i, SPOT[i], 0) for i in range(NZ))
    slot = spot * CAP + rank

    prow_row = jnp.broadcast_to((prow[...] + 1).astype(F32), (8, RO)).astype(BF16)
    meta = []
    for i, k in enumerate(SIDES):
        to = dest_x == lax.rem(x + k, NX)
        pack[i] = equal(iota((NZ * CAP, RO), 0), jnp.where(to, slot, -1))
        msend[i] = nt(prow_row, pack[i])
        meta.append(remote(msend.at[i], mrecv.at[i], ms, mr.at[i], at_x(k)))
        meta[-1].start()

    oz = equal(iota((NZ, RO), 0), spot)
    counts = []
    for kind in (OWN, OPP):
        to = dest_x == lax.rem(x + 2 * kind, NX)
        key = jnp.where(to, spot * PROWS + prow[...], -1)
        sel[kind] = equal(iota((NZ * PROWS, RO), 0), key)
        counts.append(nt(oz, equal(iota((LANES, RO), 0), jnp.where(to, prow[...], -1))))

    offset = iota((LANES, 3 * LANES), 0) - iota((LANES, 3 * LANES), 1) + (LANES + (TAPS - 1) // 2)
    for copy in mat_loads:
        copy.wait()
    band = jnp.zeros((LANES, 3 * LANES), F32)
    tap = taps[...].astype(F32)
    for t in range(TAPS):
        band = jnp.where(offset == t, jnp.broadcast_to(tap[:, t : t + 1], (LANES, 3 * LANES)), band)
    band = band.astype(BF16)
    for b in range(NC):
        low, high = max(b - 1, 0), min(b + 2, NC)
        strip = band[:, (low - b + 1) * LANES : (high - b + 1) * LANES]
        mat[b * LANES : (b + 1) * LANES, :] = mm(strip, cw[low * LANES : high * LANES, :]).astype(BF16)

    piece_load.wait()
    row_load.wait()
    for copy in halo:
        copy.wait_recv()
    off_next = last - halo_in[0][0:1]
    off_prev = halo_in[1][0:1] - first
    shift = -0.5 * off_next + 0.5 * off_prev

    def x_copy(g, i):
        source, target = (xsend[g].at[i], xrecv[g].at[i]) if i < 2 else (ysend[g], yrecv[g])
        return remote(source, target, (xs if i < 2 else ys).at[g], xr.at[g, i], at_x(SIDES[i]))

    def rows_of(n):
        return pl.ds(0, UNITS[n][3])

    def chain_copy(n, chain, step):
        direction, left, m = chain
        hop, rows = left[step] - left[step + 1], rows_of(n)
        source = ring[n].at[m + step - 1, rows] if step else acc[n].at[spot_of(chain, 0), rows]
        return remote(source, ring[n].at[m + step, rows], rs.at[n], rr.at[n, m + step], at_z(hop if direction == 0 else -hop))

    def chain_step(n, c, step):
        chain = chains(n)[c]
        if step:
            chain_copy(n, chain, step - 1).wait_recv()
            ring[n][chain[2] + step - 1, rows_of(n)] += acc[n][spot_of(chain, step), rows_of(n)]
        chain_copy(n, chain, step).start()

    def chain_total(n):
        total = acc[n][SPOT[0], rows_of(n)]
        for chain in chains(n):
            last = len(chain[1]) - 2
            chain_copy(n, chain, last).wait_recv()
            total += ring[n][chain[2] + last, rows_of(n)]
        return total

    def opp_copy(n):
        rows, o = rows_of(n), n - NOWN
        return remote(osend[o].at[rows], orecv[o].at[rows], os.at[o], oR.at[o], at_x(2))

    def opp_last(n):
        osend[n - NOWN][rows_of(n), :] = chain_total(n)
        opp_copy(n).start()

    def spread(packed, i):
        at = packed[0:1].astype(I32)
        lane = iota((1, NZ * CAP), 1) // CAP
        key = jnp.where(at > 0, lane * PROWS + at - 1, -1)
        for g, (low, high) in enumerate(GROUPS):
            part = key[:, low * CAP : high * CAP]
            place[g][i] = equal(iota(((high - low) * PROWS, (high - low) * CAP), 0) + low * PROWS, part)
        return nt(equal(iota((NZ, NZ * CAP), 0), lane), equal(iota((LANES, NZ * CAP), 0), at - 1))

    def columns(n):
        return slice(UNITS[n][1], UNITS[n][1] + UNITS[n][2])

    def take_packed(g):
        low, high = GROUPS[g]
        for i in (0, 1, 2):
            x_copy(g, i).wait_recv()
        for n in range(NOWN):
            shape = (high - low, PROWS, UNITS[n][2])
            total = acc[n][low:high, 0:PROWS].reshape(shape[0] * PROWS, shape[2])
            for i in (0, 1):
                total += mm(place[g][i], xrecv[g][i, :, columns(n)].astype(BF16))
            if UNITS[n][1] >= ZFIRST:
                part = slice(UNITS[n][1] - ZFIRST, UNITS[n][1] - ZFIRST + UNITS[n][2])
                total += mm(place[g][2], yrecv[g][:, part].astype(BF16))
            acc[n][low:high, 0:PROWS] = total.reshape(shape)

    def fill_counts(n, number):
        for part in range(UNITS[n][2] // LANES):
            acc[n][:, PROWS : PROWS + 1, part * LANES : (part + 1) * LANES] = number[:, None, :]

    def dense(kind, width):
        total = mm(sel[kind], wbuf[:, 0:width])
        for n in range(count):
            if UNITS[n][0] == kind:
                acc[n][:, 0:PROWS] = total[:, columns(n)].reshape(NZ, PROWS, UNITS[n][2])

    fill_counts(NOWN, counts[OPP])

    corr[...] = (ex[...] + shift).astype(BF16)
    ybuf[...] = mm(rw[...], corr[...]).astype(BF16)
    wbuf[...] = mm(ybuf[...], mat[...]).astype(BF16)
    packed = [mm(pack[i], wbuf[...] if i < 2 else wbuf[:, ZFIRST:]) for i in (0, 1, 2)]
    for g, (low, high) in enumerate(GROUPS):
        for i in (0, 1, 2):
            part = packed[i][low * CAP : high * CAP]
            if i < 2:
                xsend[g][i] = part
            else:
                ysend[g][...] = part
    for g in range(2):
        for i in (0, 1, 2):
            x_copy(g, i).start()
    dense(OPP, ZFIRST)
    for n in range(NOWN, count):
        for c in range(len(chains(n))):
            chain_step(n, c, 0)
    for g in range(2, len(GROUPS)):
        for i in (0, 1, 2):
            x_copy(g, i).start()
    dense(OWN, W)

    number = counts[OWN]
    for i in (0, 1, 2):
        meta[i].wait_recv()
        arrived = spread(mrecv[i], i)
        if i < 2:
            number += arrived
    fill_counts(0, number)

    for step in ORDER:
        if step[0] == "x":
            take_packed(step[1])
        elif step[0] == "o":
            opp_last(step[1])
        else:
            chain_step(*step)

    diag = iota((PROWS, LANES), 1) == iota((PROWS, LANES), 0)
    for n in range(NOWN, count):
        opp_copy(n).wait_recv()
    for n in range(NOWN):
        total = chain_total(n)
        if n == 0:
            number = jnp.broadcast_to(total[PROWS : PROWS + 1, 0:LANES] + orecv[0][PROWS : PROWS + 1, 0:LANES], (PROWS, LANES))
            number = jnp.maximum(jnp.sum(jnp.where(diag, number, 0.0), axis=1, keepdims=True), 1.0)
        for c in range(UNITS[n][2] // LANES):
            first_column = UNITS[n][1] + c * LANES
            other = 0.0
            for o in range(NOWN, count):
                at = first_column - UNITS[o][1]
                if 0 <= at < UNITS[o][2]:
                    other = orecv[o - NOWN][0:PROWS, at : at + LANES]
            out[:, first_column : first_column + LANES] = (total[0:PROWS, c * LANES : (c + 1) * LANES] + other) / number

    remote(halo_out, halo_in, hs, hr.at[0], prv).wait_send()
    remote(msend, mrecv, ms, mr.at[0], at_x(1)).wait_send()
    for g in range(len(GROUPS)):
        remote(xsend[g], xrecv[g], xs.at[g], xr.at[g, 0], at_x(1)).wait_send()
        x_copy(g, 2).wait_send()
    for n in range(count):
        sent = ring[n].at[:, rows_of(n)]
        remote(sent, sent, rs.at[n], rr.at[n, 0], at_z(1)).wait_send()
    for n in range(NOWN, count):
        opp_copy(n).wait_send()


def on_device(exposure, psf_taps, col_warp, row_warp, row_patch, row_prow, owner_map):
    anywhere = pl.BlockSpec(memory_space=pl.ANY)
    dma = pltpu.SemaphoreType.DMA
    vmem = pltpu.VMEM
    blocks = [(-(-rows // 8) * 8, width) for _, _, width, rows in UNITS]
    packs = [vmem((2, (high - low) * CAP, W), F32) for low, high in GROUPS]
    places = [vmem((3, (high - low) * PROWS, (high - low) * CAP), BF16) for low, high in GROUPS]
    sides = [vmem(((high - low) * CAP, W - ZFIRST), F32) for low, high in GROUPS]
    others = [vmem(block, F32) for block in blocks[NOWN:]]
    return pl.pallas_call(
        kernel,
        out_shape=vmem((PROWS, W), F32),
        in_specs=[anywhere] * 7,
        out_specs=pl.BlockSpec(memory_space=vmem),
        scratch_shapes=[
            vmem((R, W), F32),
            vmem((2, STRIP, W), F32),
            vmem((1, TAPS), BF16),
            vmem((W, W), BF16),
            vmem((RO, R), BF16),
            vmem((1, RO), I32),
            vmem((1, RO), I32),
            vmem((1, NX * NZ), I32),
            vmem((W, W), BF16),
            vmem((R, W), BF16),
            vmem((RO, W), BF16),
            vmem((RO, W), BF16),
            vmem((2, NZ * PROWS, RO), BF16),
            vmem((3, NZ * CAP, RO), BF16),
            vmem((2, 8, W), F32),
            vmem((2, 8, W), F32),
            vmem((3, 8, NZ * CAP), F32),
            vmem((3, 8, NZ * CAP), F32),
            dma((9,)),
            dma(()),
            dma((2,)),
            dma(()),
            dma((3,)),
            dma((len(GROUPS),)),
            dma((len(GROUPS),)),
            dma((len(GROUPS), 3)),
            dma((len(UNITS),)),
            dma((len(UNITS), NM)),
            dma((len(UNITS) - NOWN,)),
            dma((len(UNITS) - NOWN,)),
        ]
        + [vmem((NZ, *block), F32) for block in blocks]
        + [vmem((NM, *block), F32) for block in blocks]
        + others
        + others
        + packs
        + packs
        + places
        + sides
        + sides,
        compiler_params=pltpu.CompilerParams(collective_id=0, has_side_effects=True),
    )(
        exposure,
        psf_taps,
        col_warp,
        row_warp,
        row_patch.reshape(1, RO),
        row_prow.reshape(1, RO),
        owner_map.reshape(1, -1),
    )


def solution(mesh):
    placed = (
        P(("band", "exp"), None),
        P(("band", "exp"), None),
        P(("band", "exp"), None),
        P(("band", "exp"), None),
        P(("band", "exp"), None),
        P(("band", "exp")),
        P("band"),
    )
    return jax.shard_map(
        on_device, mesh=mesh, in_specs=placed, out_specs=P(("band", "exp"), None), check_vma=False
    )
```

```python
import functools

import jax
import jax.numpy as jnp
from jax import lax
from jax.experimental import pallas as pl
from jax.experimental.pallas import tpu as pltpu
from jax.sharding import PartitionSpec as P

F32, BF16, I32 = jnp.float32, jnp.bfloat16, jnp.int32
MESH = pl.DeviceIdType.MESH

STRIP = 16
TAPS = 15
PROWS = 32
CAP = 16
NX, NZ = 4, 16
W, R, RO = 512, 1024, 512
LANES = 128

NC = W // LANES
OWN, OPP = 0, 1
NM = NZ - 1
SIDES = (1, 3, 2)

UNITS = (
    (OWN, 0, 128, 33),
    (OWN, 128, 128, 32),
    (OWN, 256, 128, 32),
    (OWN, 384, 128, 32),
    (OPP, 0, 128, 33),
    (OPP, 128, 128, 32),
)
NOWN = sum(u[0] == OWN for u in UNITS)
ZFIRST = 256
XTILES = 3 * NC - ZFIRST // LANES
NEAR = (2, 2)
SPOT = (15, 13, 7, 11, 9, 5, 3, 1, 0, 2, 4, 6, 10, 12, 8, 14)
GROUPS = ((0, 1), (1, 3), (3, 5), (5, 7), (7, 9), (9, 11), (11, 13), (13, 16))
ORDER = (
    (4, 0, 1), (4, 2, 1), (4, 1, 1), (4, 3, 1), ("x", 0), (5, 2, 1), (0, 0, 0), (1, 2, 0), (2, 0, 0), (3, 2, 0),
    (5, 0, 1), (5, 1, 1), (5, 3, 1), ("x", 1), (0, 2, 0), (1, 0, 0), (2, 2, 0), (3, 0, 0), (4, 0, 2), (4, 2, 2),
    (5, 2, 2), (0, 0, 1), (1, 2, 1), (2, 0, 1), (3, 2, 1), (5, 0, 2), ("x", 2), (1, 0, 1), (0, 2, 1), (3, 0, 1),
    (2, 2, 1), (4, 0, 3), (4, 2, 3), ("x", 3), (5, 2, 3), (0, 0, 2), (1, 2, 2), (2, 0, 2), (3, 2, 2), (5, 0, 3),
    ("x", 4), (0, 1, 0), (1, 0, 2), (0, 3, 0), (0, 2, 2), (1, 1, 0), (1, 3, 0), (2, 1, 0), (2, 3, 0), (3, 1, 0),
    (3, 3, 0), (3, 0, 2), (2, 2, 2), (4, 0, 4), (4, 2, 4), (5, 2, 4), (0, 0, 3), (1, 2, 3), (2, 0, 3), (3, 2, 3),
    (5, 0, 4), ("x", 5), (1, 0, 3), (0, 2, 3), ("x", 6), (3, 0, 3), (2, 2, 3), (4, 0, 5), (0, 0, 4), (2, 0, 4),
    (5, 2, 5), (1, 2, 4), (3, 2, 4), ("x", 7), (1, 0, 4), (0, 1, 1), (0, 3, 1), (0, 2, 4), (1, 1, 1), (1, 3, 1),
    (2, 1, 1), (2, 3, 1), (3, 1, 1), (3, 3, 1), (3, 0, 4), (2, 2, 4), (0, 0, 5), (2, 0, 5), (1, 2, 5), (3, 2, 5),
    ("o", 4), ("o", 5),
)


def chains(n):
    out, m, near = [], 0, NEAR[UNITS[n][0]]
    for direction in (0, 1):
        far = NZ // 2 if (n + direction) % 2 == 0 else NZ // 2 - 1
        for top, bottom in ((far, near), (near, 0)) if near else ((far, 0),):
            left = (*range(top, bottom, -1), 0)
            out.append((direction, left, m))
            m += len(left) - 1
    return out


def spot_of(chain, step):
    direction, left, _ = chain
    return SPOT[left[step] if direction == 0 else NZ - left[step]]


def nt(a, b):
    return lax.dot_general(a, b, (((1,), (1,)), ((), ())), preferred_element_type=F32)


def mm(a, b):
    return jnp.dot(a, b, preferred_element_type=F32)


def iota(shape, dim):
    return lax.broadcasted_iota(I32, shape, dim)


def equal(a, b):
    return jnp.where(a == b, 1.0, 0.0).astype(BF16)


def kernel(
    expo, taps_hbm, cw_hbm, rw_hbm, patch_hbm, prow_hbm, owner_hbm, out,
    ex, strips, taps, cw, rw, patch, prow, owner, mat, corr, ybuf, wbuf, sel, pack, halo_out, halo_in,
    msend, mrecv, xsend, xrecv, in_sem, hs, hr, ms, mr, xs, xr, rs, rr, os, oR, *buffers,
):
    buffers = list(buffers)

    def take(number):
        return [buffers.pop(0) for _ in range(number)]

    count = len(UNITS)
    acc, ring, osend, orecv = take(count), take(count), take(count - NOWN), take(count - NOWN)
    place = take(len(GROUPS))
    e = lax.axis_index("exp")
    x, z = e // NZ, lax.rem(e, NZ)

    def dev(i):
        return {"exp": i}

    def at_z(d):
        return x * NZ + lax.rem(z + d + NZ, NZ)

    def at_x(d):
        return lax.rem(x + d + NX, NX) * NZ + z

    def remote(src, dst, s, r, target):
        return pltpu.make_async_remote_copy(
            src_ref=src, dst_ref=dst, send_sem=s, recv_sem=r, device_id=dev(target), device_id_type=MESH
        )

    nxt, prv = lax.rem(e + 1, NX * NZ), lax.rem(e + NX * NZ - 1, NX * NZ)

    loads = []

    def load(src, dst):
        copy = pltpu.make_async_copy(src, dst, in_sem.at[len(loads)])
        copy.start()
        loads.append(copy)
        return copy

    strip_loads = [load(expo.at[pl.ds(0, STRIP)], strips.at[0]), load(expo.at[pl.ds(R - STRIP, STRIP)], strips.at[1])]
    barrier = pltpu.get_barrier_semaphore()
    peers = [nxt, prv, at_z(1), at_z(-1), at_x(1), at_x(3), at_x(2)]
    for hop in sorted({near + 1 for near in NEAR if near}):
        peers += [at_z(hop), at_z(-hop)]
    for peer in peers:
        pl.semaphore_signal(barrier, inc=1, device_id=dev(peer), device_id_type=MESH)
    key_loads = [load(owner_hbm, owner), load(patch_hbm, patch), load(prow_hbm, prow)]
    piece_load = load(expo, ex)
    row_load = load(rw_hbm, rw)
    mat_loads = [load(taps_hbm, taps), load(cw_hbm, cw)]

    for copy in strip_loads:
        copy.wait()

    def means(strip):
        total = jnp.sum(strip, axis=0, keepdims=True)
        parts = [
            jnp.broadcast_to(
                jnp.sum(total[:, b * LANES : (b + 1) * LANES], axis=1, keepdims=True) * (1.0 / (STRIP * LANES)), (1, LANES)
            )
            for b in range(NC)
        ]
        return jnp.concatenate(parts, axis=1)

    first, last = means(strips[0]), means(strips[1])
    halo_out[0] = jnp.broadcast_to(first, (8, W))
    halo_out[1] = jnp.broadcast_to(last, (8, W))
    pl.semaphore_wait(barrier, len(peers))
    halo = [
        remote(halo_out.at[0], halo_in.at[0], hs, hr, prv),
        remote(halo_out.at[1], halo_in.at[1], hs, hr, nxt),
    ]
    for copy in halo:
        copy.start()

    for copy in key_loads:
        copy.wait()
    eye = iota((NX * NZ, NX * NZ), 0) == iota((NX * NZ, NX * NZ), 1)
    owner_col = jnp.sum(jnp.where(eye, jnp.broadcast_to(owner[...], eye.shape), 0), axis=1, keepdims=True)
    own_of = owner_col == patch[...]
    dest = jnp.sum(jnp.where(own_of, iota((NX * NZ, RO), 0), 0), axis=0, keepdims=True)
    dest_x, dest_z = dest // NZ, lax.rem(dest, NZ)
    one_hot = jnp.where(own_of, 1.0, 0.0)
    before = jnp.where(iota((RO, RO), 0) < iota((RO, RO), 1), 1.0, 0.0).astype(BF16)
    earlier = mm(one_hot.astype(BF16), before)
    rank = jnp.sum(one_hot * earlier, axis=0, keepdims=True).astype(I32)
    away = lax.rem(dest_z - z + NZ, NZ)
    spot = sum(jnp.where(away == i, SPOT[i], 0) for i in range(NZ))
    slot = spot * CAP + rank

    prow_row = jnp.broadcast_to((prow[...] + 1).astype(F32), (8, RO)).astype(BF16)
    meta = []
    for i, k in enumerate(SIDES):
        to = dest_x == lax.rem(x + k, NX)
        pack[i] = equal(iota((NZ * CAP, RO), 0), jnp.where(to, slot, -1))
        msend[i] = nt(prow_row, pack[i])
        meta.append(remote(msend.at[i], mrecv.at[i], ms, mr, at_x(k)))
        meta[-1].start()

    oz = equal(iota((NZ, RO), 0), spot)
    counts = []
    for kind in (OWN, OPP):
        to = dest_x == lax.rem(x + 2 * kind, NX)
        key = jnp.where(to, spot * PROWS + prow[...], -1)
        sel[kind] = equal(iota((NZ * PROWS, RO), 0), key)
        counts.append(nt(oz, equal(iota((LANES, RO), 0), jnp.where(to, prow[...], -1))))

    offset = iota((LANES, 3 * LANES), 0) - iota((LANES, 3 * LANES), 1) + (LANES + (TAPS - 1) // 2)
    for copy in mat_loads:
        copy.wait()
    band = jnp.zeros((LANES, 3 * LANES), F32)
    tap = taps[...].astype(F32)
    for t in range(TAPS):
        band = jnp.where(offset == t, jnp.broadcast_to(tap[:, t : t + 1], (LANES, 3 * LANES)), band)
    band = band.astype(BF16)
    for b in range(NC):
        low, high = max(b - 1, 0), min(b + 2, NC)
        strip = band[:, (low - b + 1) * LANES : (high - b + 1) * LANES]
        mat[b * LANES : (b + 1) * LANES, :] = mm(strip, cw[low * LANES : high * LANES, :]).astype(BF16)

    piece_load.wait()
    row_load.wait()
    remote(halo_out, halo_in, hs, hr, prv).wait_recv()
    off_next = last - halo_in[0][0:1]
    off_prev = halo_in[1][0:1] - first
    shift = -0.5 * off_next + 0.5 * off_prev

    def x_part(g, i):
        low, high = GROUPS[g]
        return pl.ds(i * NC, NC if i < 2 else XTILES - 2 * NC), pl.ds(low * CAP, (high - low) * CAP)

    def x_copy(g, i):
        part = x_part(g, i)
        return remote(xsend.at[part], xrecv.at[part], xs, xr.at[g], at_x(SIDES[i]))

    def x_wait(g):
        part = xrecv.at[:, x_part(g, 0)[1]]
        remote(part, part, xs, xr.at[g], at_x(1)).wait_recv()

    def rows_of(n):
        return pl.ds(0, UNITS[n][3])

    def chain_copy(n, chain, step):
        direction, left, m = chain
        hop, rows = left[step] - left[step + 1], rows_of(n)
        source = ring[n].at[m + step - 1, rows] if step else acc[n].at[spot_of(chain, 0), rows]
        return remote(source, ring[n].at[m + step, rows], rs.at[n], rr.at[n, m + step], at_z(hop if direction == 0 else -hop))

    def chain_step(n, c, step):
        chain = chains(n)[c]
        if step:
            chain_copy(n, chain, step - 1).wait_recv()
            ring[n][chain[2] + step - 1, rows_of(n)] += acc[n][spot_of(chain, step), rows_of(n)]
        chain_copy(n, chain, step).start()

    def chain_total(n):
        total = acc[n][SPOT[0], rows_of(n)]
        for chain in chains(n):
            last = len(chain[1]) - 2
            chain_copy(n, chain, last).wait_recv()
            total += ring[n][chain[2] + last, rows_of(n)]
        return total

    def opp_copy(n):
        rows, o = rows_of(n), n - NOWN
        return remote(osend[o].at[rows], orecv[o].at[rows], os.at[o], oR.at[o], at_x(2))

    def opp_last(n):
        osend[n - NOWN][rows_of(n), :] = chain_total(n)
        opp_copy(n).start()

    def spread(packed, i):
        at = packed[0:1].astype(I32)
        lane = iota((1, NZ * CAP), 1) // CAP
        key = jnp.where(at > 0, lane * PROWS + at - 1, -1)
        for g, (low, high) in enumerate(GROUPS):
            part = key[:, low * CAP : high * CAP]
            place[g][i] = equal(iota(((high - low) * PROWS, (high - low) * CAP), 0) + low * PROWS, part)
        return nt(equal(iota((NZ, NZ * CAP), 0), lane), equal(iota((LANES, NZ * CAP), 0), at - 1))

    def columns(n):
        return slice(UNITS[n][1], UNITS[n][1] + UNITS[n][2])

    def take_packed(g):
        low, high = GROUPS[g]
        slots = slice(low * CAP, high * CAP)
        x_wait(g)
        for n in range(NOWN):
            shape = (high - low, PROWS, UNITS[n][2])
            total = acc[n][low:high, 0:PROWS].reshape(shape[0] * PROWS, shape[2])
            first_tile, tiles = UNITS[n][1] // LANES, UNITS[n][2] // LANES
            for i in (0, 1, 2):
                if i == 2 and UNITS[n][1] < ZFIRST:
                    continue
                at = i * NC + first_tile - (ZFIRST // LANES if i == 2 else 0)
                arrived = [xrecv[at + tile, slots] for tile in range(tiles)]
                arrived = arrived[0] if tiles == 1 else jnp.concatenate(arrived, axis=1)
                total += mm(place[g][i], arrived.astype(BF16))
            acc[n][low:high, 0:PROWS] = total.reshape(shape)

    def fill_counts(n, number):
        for part in range(UNITS[n][2] // LANES):
            acc[n][:, PROWS : PROWS + 1, part * LANES : (part + 1) * LANES] = number[:, None, :]

    def dense(kind, width):
        total = mm(sel[kind], wbuf[:, 0:width])
        for n in range(count):
            if UNITS[n][0] == kind:
                acc[n][:, 0:PROWS] = total[:, columns(n)].reshape(NZ, PROWS, UNITS[n][2])

    fill_counts(NOWN, counts[OPP])

    corr[...] = (ex[...] + shift).astype(BF16)
    ybuf[...] = mm(rw[...], corr[...]).astype(BF16)
    wbuf[...] = mm(ybuf[...], mat[...]).astype(BF16)
    packed = [mm(pack[i], wbuf[...] if i < 2 else wbuf[:, ZFIRST:]) for i in (0, 1, 2)]
    for i in (0, 1, 2):
        for tile in range(NC if i < 2 else XTILES - 2 * NC):
            xsend[i * NC + tile] = packed[i][:, tile * LANES : (tile + 1) * LANES]
    for g in range(2):
        for i in (0, 1, 2):
            x_copy(g, i).start()
    dense(OPP, ZFIRST)
    for n in range(NOWN, count):
        for c in range(len(chains(n))):
            chain_step(n, c, 0)
    for g in range(2, len(GROUPS)):
        for i in (0, 1, 2):
            x_copy(g, i).start()
    dense(OWN, W)

    number = counts[OWN]
    remote(msend, mrecv, ms, mr, at_x(1)).wait_recv()
    for i in (0, 1, 2):
        arrived = spread(mrecv[i], i)
        if i < 2:
            number += arrived
    fill_counts(0, number)

    for step in ORDER:
        if step[0] == "x":
            take_packed(step[1])
        elif step[0] == "o":
            opp_last(step[1])
        else:
            chain_step(*step)

    diag = iota((PROWS, LANES), 1) == iota((PROWS, LANES), 0)
    for n in range(NOWN, count):
        opp_copy(n).wait_recv()
    for n in range(NOWN):
        total = chain_total(n)
        if n == 0:
            number = jnp.broadcast_to(total[PROWS : PROWS + 1, 0:LANES] + orecv[0][PROWS : PROWS + 1, 0:LANES], (PROWS, LANES))
            number = jnp.maximum(jnp.sum(jnp.where(diag, number, 0.0), axis=1, keepdims=True), 1.0)
        for c in range(UNITS[n][2] // LANES):
            first_column = UNITS[n][1] + c * LANES
            other = 0.0
            for o in range(NOWN, count):
                at = first_column - UNITS[o][1]
                if 0 <= at < UNITS[o][2]:
                    other = orecv[o - NOWN][0:PROWS, at : at + LANES]
            out[:, first_column : first_column + LANES] = (total[0:PROWS, c * LANES : (c + 1) * LANES] + other) / number

    remote(halo_out, halo_in, hs, hr, prv).wait_send()
    remote(msend, mrecv, ms, mr, at_x(1)).wait_send()
    remote(xsend, xrecv, xs, xr.at[0], at_x(1)).wait_send()
    for n in range(count):
        sent = ring[n].at[:, rows_of(n)]
        remote(sent, sent, rs.at[n], rr.at[n, 0], at_z(1)).wait_send()
    for n in range(NOWN, count):
        opp_copy(n).wait_send()


def on_device(exposure, psf_taps, col_warp, row_warp, row_patch, row_prow, owner_map):
    anywhere = pl.BlockSpec(memory_space=pl.ANY)
    dma = pltpu.SemaphoreType.DMA
    vmem = pltpu.VMEM
    blocks = [(-(-rows // 8) * 8, width) for _, _, width, rows in UNITS]
    places = [vmem((3, (high - low) * PROWS, (high - low) * CAP), BF16) for low, high in GROUPS]
    others = [vmem(block, F32) for block in blocks[NOWN:]]
    return pl.pallas_call(
        kernel,
        out_shape=vmem((PROWS, W), F32),
        in_specs=[anywhere] * 7,
        out_specs=pl.BlockSpec(memory_space=vmem),
        scratch_shapes=[
            vmem((R, W), F32),
            vmem((2, STRIP, W), F32),
            vmem((1, TAPS), BF16),
            vmem((W, W), BF16),
            vmem((RO, R), BF16),
            vmem((1, RO), I32),
            vmem((1, RO), I32),
            vmem((1, NX * NZ), I32),
            vmem((W, W), BF16),
            vmem((R, W), BF16),
            vmem((RO, W), BF16),
            vmem((RO, W), BF16),
            vmem((2, NZ * PROWS, RO), BF16),
            vmem((3, NZ * CAP, RO), BF16),
            vmem((2, 8, W), F32),
            vmem((2, 8, W), F32),
            vmem((3, 8, NZ * CAP), F32),
            vmem((3, 8, NZ * CAP), F32),
            vmem((XTILES, NZ * CAP, LANES), F32),
            vmem((XTILES, NZ * CAP, LANES), F32),
            dma((9,)),
            dma(()),
            dma(()),
            dma(()),
            dma(()),
            dma(()),
            dma((len(GROUPS),)),
            dma((len(UNITS),)),
            dma((len(UNITS), NM)),
            dma((len(UNITS) - NOWN,)),
            dma((len(UNITS) - NOWN,)),
        ]
        + [vmem((NZ, *block), F32) for block in blocks]
        + [vmem((NM, *block), F32) for block in blocks]
        + others
        + others
        + places,
        compiler_params=pltpu.CompilerParams(collective_id=0, has_side_effects=True),
    )(
        exposure,
        psf_taps,
        col_warp,
        row_warp,
        row_patch.reshape(1, RO),
        row_prow.reshape(1, RO),
        owner_map.reshape(1, -1),
    )


def solution(mesh):
    placed = (
        P(("band", "exp"), None),
        P(("band", "exp"), None),
        P(("band", "exp"), None),
        P(("band", "exp"), None),
        P(("band", "exp"), None),
        P(("band", "exp")),
        P("band"),
    )
    return jax.shard_map(
        on_device, mesh=mesh, in_specs=placed, out_specs=P(("band", "exp"), None), check_vma=False
    )
```
